128 devices in a mesh: inp: 4 (over z_lo, core), chan: 32 (over z_hi, x, y).
Axes of the slice: x: 4, y: 4, z: 4 (z_hi: 2, z_lo: 2; z = z_hi * 2 + z_lo), core: 2. Of those that a mesh axis runs over, the one named last changes fastest.
Arguments:
- voltages: bfloat16 [1024, 1048576], P('inp', 'chan'), may hold values from -4 to 4
- scale_codes: int32 [1024], P('inp'), may hold values from 4 to 32
- kept_channels: int32 [128], replicated, may hold values from 0 to 4095, as said below
Outputs:
- visibilities: float32 [2, 128, 1024, 1024], P(None, 'chan', 'inp')
The draws below stay inside these ranges and needn't reach their ends.
Inputs may be any that keep to these rules, and one draw needn't show every extreme that they name: `kept_channels`: 128 distinct channel numbers.
All inputs are finite; a program needn't handle non-finite values.
Results may differ from the reference program's by a relative error of at most 0.0036.
Values may be sent and summed in bfloat16 or wider, within the bound.
A program may use at most 384 MiB of HBM per device.

```python
import jax
import jax.numpy as jnp
from jax import lax

INPUTS = 1024
TRANSFORM = 8192
CHANNELS = 4096
KEPT = 128
TAPS = 4
SPECTRA = 128
SAMPLES = 1048576


def draw_kept_channels(key, part):
    middle = jax.random.permutation(key, CHANNELS - 2)[:KEPT - 2].astype(jnp.int32) + 1
    whole = jnp.concatenate([jnp.zeros((1,), jnp.int32), middle, jnp.full((1,), CHANNELS - 1, jnp.int32)])
    order = jax.random.permutation(jax.random.fold_in(key, 7), KEPT)
    return whole[order].astype(jnp.int32)


def plant(entries, stream_key, smallest, top_value):
    longest = entries.shape.index(max(entries.shape))
    spots = []
    for shift in (0, 1):
        where = [jax.random.randint(jax.random.fold_in(stream_key, axis), (), 0, length) for axis, length in enumerate(entries.shape)]
        where[longest] = (where[longest] + shift) % entries.shape[longest]
        spots.append(tuple(where))
    return entries.at[spots[0]].set(smallest).at[spots[1]].set(top_value)


def levels(rng, extent, cuts, smallest, top_value):
    loudness = 1.0
    for dim, parts in cuts:
        steps = jax.random.uniform(jax.random.fold_in(jax.random.fold_in(rng, 6), dim), (parts,), jnp.float32, smallest / len(cuts), top_value / len(cuts))
        loudness = loudness * jnp.repeat(jnp.exp(steps), extent[dim] // parts).reshape((-1,) + (1,) * (len(extent) - 1 - dim))
    return loudness


def gaussian(own_key, shape, width, limit, split=(), held_as=jnp.bfloat16):
    array = jax.random.normal(own_key, shape, jnp.float32) * width
    if len(split) > 0:
        array = levels(own_key, shape, split, -0.22, 0.18) * array
    return jnp.clip(array, min=-limit, max=limit).astype(held_as)


def setup_inputs(seed: int = 0) -> dict:
    key_list = jax.random.split(jax.random.key(seed), 4)
    return {
        "voltages": gaussian(key_list[0], (INPUTS, SAMPLES), 1.0, 4.0, ((0, 4), (1, 32))),
        "scale_codes": plant(jax.random.randint(key_list[1], (INPUTS,), 4, 33), jax.random.fold_in(key_list[1], 1), 4, 32).astype(jnp.int32),
        "kept_channels": draw_kept_channels(jax.random.fold_in(key_list[3], 71), 0),
    }


def prototype():
    sample = jnp.arange(TAPS * TRANSFORM, dtype=jnp.float32)
    offset = (sample + 0.5) / TRANSFORM - TAPS / 2.0
    window = 0.5 - 0.5 * jnp.cos(2.0 * jnp.pi * (sample + 0.5) / (TAPS * TRANSFORM))
    return (jnp.sinc(offset) * window).reshape(TAPS, TRANSFORM)

def reference(voltages, scale_codes, kept_channels):
    coeffs = prototype()
    groups = voltages.reshape(INPUTS // 32, 32, SPECTRA, TRANSFORM)
    code_groups = scale_codes.reshape(INPUTS // 32, 32)

    def channelize(operands):
        group_in, code_group = operands
        samples = group_in.astype(jnp.float32)
        padded = jnp.pad(samples, ((0, 0), (TAPS - 1, 0), (0, 0)))
        filtered = sum((coeffs[tap_index] * padded[:, tap_index:tap_index + SPECTRA] for tap_index in range(TAPS)))
        spectrum = jnp.fft.rfft(filtered, axis=-1)[..., kept_channels] / jnp.sqrt(jnp.float32(TRANSFORM))
        stacked = jnp.stack([jnp.real(spectrum), jnp.imag(spectrum)], axis=-1)
        scales = code_group.astype(jnp.float32) / 16.0
        return (stacked * scales[:, None, None, None]).astype(jnp.bfloat16)
    channelized = lax.map(channelize, (groups, code_groups)).reshape(INPUTS, SPECTRA, KEPT, 2)

    def correlate(channel):
        column = lax.dynamic_index_in_dim(channelized, channel, axis=2, keepdims=False)
        rows = column.reshape(INPUTS, 2 * SPECTRA)
        rotated = jnp.stack([-column[..., 1], column[..., 0]], axis=-1).reshape(INPUTS, 2 * SPECTRA)
        real_part = jnp.dot(rows, rows.T, preferred_element_type=jnp.float32)
        imag_part = jnp.dot(rows, rotated.T, preferred_element_type=jnp.float32)
        return jnp.stack([real_part, imag_part]) / SPECTRA
    result = lax.map(correlate, jnp.arange(KEPT, dtype=jnp.int32))
    return jnp.moveaxis(result, 1, 0)
```

```python
import functools, numpy as np
import jax, jax.numpy as jnp
from jax import lax
from jax.experimental import pallas as pl
from jax.experimental.pallas import tpu as pltpu
from jax.sharding import PartitionSpec as P
N=8192; TAPS=4
KC=512
STEPS=N//(2*KC)
AC=KC//128
f32=jnp.float32; bf16=jnp.bfloat16

def prototype():
    m=np.arange(TAPS*N,dtype=np.float64)
    u=(m+.5)/N-TAPS/2
    w=0.5-0.5*np.cos(2*np.pi*(m+.5)/(TAPS*N))
    return (np.sinc(u)*w).reshape(TAPS,N).astype(np.float32)

def trig(kept):
    k=jnp.repeat(kept,2)
    ph=jnp.tile(jnp.array([0,N//4],jnp.int32),kept.shape[0])
    b=jnp.arange(128,dtype=jnp.int32)
    a=jnp.arange(64,dtype=jnp.int32)
    beta=(k[:,None]*b[None]+ph[:,None])%N
    alpha=(k[:,None]*(a*128)[None])%N
    w=2*np.pi/N
    beta=beta.astype(f32)*w; alpha=alpha.astype(f32)*w
    return jnp.cos(alpha),jnp.sin(alpha),jnp.cos(beta),jnp.sin(beta)

def gen(dst, ca, sa, a0, cb, sb, cref, c0):
    for i in range(AC):
        for r in range(0,256,32):
            A=ca[r:r+32,a0+i:a0+i+1]; S=sa[r:r+32,a0+i:a0+i+1]
            base=A*cb[r:r+32,:]-S*sb[r:r+32,:]
            for t in range(TAPS):
                co=cref[t:t+1,c0+i*128:c0+(i+1)*128]
                dst[t,r:r+32,i*128:(i+1)*128]=(base*co).astype(bf16)

def dots(T, vs, c0, acc):
    for q in range(7):
        s=None
        for f in range(4):
            t=f+3-q
            if 0<=t<4:
                d=lax.dot_general(T[t],vs[f][:,c0:c0+KC],(((1,),(1,)),((),())),preferred_element_type=f32)
                s=d if s is None else s+d
        acc[q]+=s

def front_kernel(v0,v1,v2,v3,ca,sa,cb,sb,co,cap,sap,cop,scale,own,halo,T0,T1,acc):
    g=pl.program_id(0)
    vs=(v0,v1,v2,v3)
    @pl.when(g==0)
    def _():
        acc[...]=jnp.zeros_like(acc)
        gen(T0,cap,sap,0,cb,sb,cop,0)
    gen(T1,ca.at[0],sa.at[0],0,cb,sb,co,0)
    dots(T0,vs,0,acc)
    gen(T0,ca.at[0],sa.at[0],AC,cb,sb,co,KC)
    dots(T1,vs,KC,acc)
    @pl.when(g==STEPS-1)
    def _():
        sc=scale[...]
        for q in range(1,5): own[q-1]=acc[q]*sc
        for i,q in enumerate((5,6,0)): halo[i]=(acc[q]*sc).astype(bf16)

def front(volt, scale_codes, kept):
    CA,SA,CB,SB=trig(kept)
    def shift3(x):
        x=jnp.roll(x,-AC,axis=1)
        return x.reshape(256,STEPS,2*AC).transpose(1,0,2)
    c=prototype()
    cs=jnp.asarray(np.roll(c,-KC,axis=1))
    scale=(scale_codes.astype(f32)*np.float32(1/16/np.sqrt(N)))[None,:]
    vspec=[pl.BlockSpec((256,2*KC),functools.partial(lambda f,g:(0,f*STEPS+g),f)) for f in range(4)]
    full=lambda s: pl.BlockSpec(s,lambda g:(0,)*len(s))
    aspec=pl.BlockSpec((1,256,2*AC),lambda g:(g,0,0))
    return pl.pallas_call(front_kernel,
        grid=(STEPS,),
        in_specs=vspec+[aspec,aspec,full((256,128)),full((256,128)),pl.BlockSpec((4,2*KC),lambda g:(0,g)),
            full((256,AC)),full((256,AC)),full((4,KC)),full((1,256))],
        out_specs=[full((4,256,256)),full((3,256,256))],
        out_shape=[jax.ShapeDtypeStruct((4,256,256),f32),jax.ShapeDtypeStruct((3,256,256),bf16)],
        scratch_shapes=[pltpu.VMEM((4,256,KC),bf16),pltpu.VMEM((4,256,KC),bf16),pltpu.VMEM((7,256,256),f32)],
        compiler_params=pltpu.CompilerParams(vmem_limit_bytes=60000*1024),
        name="front",
    )(volt,volt,volt,volt,shift3(CA),shift3(SA),CB,SB,cs,CA[:,:AC],SA[:,:AC],jnp.asarray(c[:,:KC]),scale)


def assemble_kernel(own,fwd,bwd,mask,out,W):
    parts=(own[0]+fwd[0].astype(f32),own[1]+fwd[1].astype(f32),own[2],own[3]*mask[...]+bwd[...].astype(f32))
    for s in range(4):
        for h in range(2):
            W[h,pl.ds(s,256,stride=4),:]=parts[s][:,h*128:(h+1)*128]
    for h in range(2):
        out[:,:,h*128:(h+1)*128]=W[h].astype(bf16).reshape(32,32,128)

def assemble(own,fwd,bwd,mask):
    return pl.pallas_call(assemble_kernel,
        out_shape=jax.ShapeDtypeStruct((32,32,256),bf16),
        scratch_shapes=[pltpu.VMEM((2,1024,128),f32)],
        compiler_params=pltpu.CompilerParams(vmem_limit_bytes=32*1024*1024),
        name="assemble")(own,fwd,bwd,mask)

def correlate_kernel(mine,every,out):
    a=mine[...].astype(f32)
    turned=jnp.concatenate([a[:,4:],-a[:,:4]],axis=1)
    both=jnp.concatenate([a.reshape(256,256),turned.reshape(256,256)],axis=1).astype(bf16)
    for i in range(4):
        b=every[i].astype(f32).reshape(256,256).astype(bf16)
        d=lax.dot_general(both,b,(((0,),(0,)),((),())),preferred_element_type=f32)*np.float32(1/128)
        out[0,0,:,i*256:(i+1)*256]=d[:256]
        out[1,0,:,i*256:(i+1)*256]=d[256:]

def correlate(mine,every):
    return pl.pallas_call(correlate_kernel,
        grid=(4,),
        in_specs=[pl.BlockSpec((32,8,256),lambda j:(0,j,0)),pl.BlockSpec((4,32,8,256),lambda j:(0,0,j,0))],
        out_specs=pl.BlockSpec((2,1,256,1024),lambda j:(0,j,0,0)),
        out_shape=jax.ShapeDtypeStruct((2,4,256,1024),f32),
        compiler_params=pltpu.CompilerParams(vmem_limit_bytes=40*1024*1024),
        name="correlate")(mine,every)


def copy_for_each(shard,axis):
    copies=jnp.broadcast_to(shard,(lax.axis_size(axis),*shard.shape))
    return lax.all_to_all(copies,axis,split_axis=0,concat_axis=0,tiled=True)

def local(voltages,scale_codes,kept_channels):
    own,halo=front(voltages,scale_codes,kept_channels)
    me=lax.axis_index("chan")
    size=lax.axis_size("chan")
    fwd=lax.ppermute(halo[:2],"chan",[(i,i+1) for i in range(size-1)])
    bwd=lax.ppermute(halo[2],"chan",[(i,(i+size-1)%size) for i in range(size)])
    mask=jnp.full((1,256),jnp.where(me==size-1,0.0,1.0),f32)
    mine=assemble(own,fwd,bwd,mask)
    turned=lax.all_to_all(mine,"chan",split_axis=0,concat_axis=0,tiled=True)
    every=copy_for_each(turned,"inp")
    return correlate(turned,every)

def solution(mesh):
    placed=(P("inp","chan"),P("inp"),P())
    return jax.shard_map(local,mesh=mesh,in_specs=placed,out_specs=P(None,"chan","inp",None),check_vma=False)
```

```python
import functools, numpy as np
import jax, jax.numpy as jnp
from jax import lax
from jax.experimental import pallas as pl
from jax.experimental.pallas import tpu as pltpu
from jax.sharding import PartitionSpec as P
N=8192; TAPS=4
G=1; KC=512; MODE='sep'
R=256//G; H=R//2
STEPS=N//(2*KC)
AC=KC//128
f32=jnp.float32; bf16=jnp.bfloat16

def prototype():
    m=np.arange(TAPS*N,dtype=np.float64)
    u=(m+.5)/N-TAPS/2
    w=0.5-0.5*np.cos(2*np.pi*(m+.5)/(TAPS*N))
    return (np.sinc(u)*w).reshape(TAPS,N).astype(np.float32)

def cos_sin(m):
    quad=(m+N//8)//(N//4)
    x=(m-quad*(N//4)).astype(f32)*np.float32(2*np.pi/N)
    y=x*x
    c=1.0+y*(-0.5+y*(1/24+y*(-1/720+y*(1/40320))))
    s=x*(1.0+y*(-1/6+y*(1/120+y*(-1/5040+y*(1/362880)))))
    quad=quad&3
    odd=(quad&1)==1
    cc=jnp.where(odd,s,c); ss=jnp.where(odd,c,s)
    cc=jnp.where((quad==1)|(quad==2),-cc,cc)
    ss=jnp.where(quad>=2,-ss,ss)
    return cc,ss

def init_tables(kept,ca,sa,cb,sb):
    kt=jnp.transpose(jnp.broadcast_to(kept[...].astype(f32),(128,128))).astype(jnp.int32)
    lane=lax.broadcasted_iota(jnp.int32,(128,128),1)
    A=(kt*((lane&63)*128))&(N-1)
    B=(kt*lane)&(N-1)
    cA,sA=cos_sin(A)
    for p in range(2):
        cB,sB=cos_sin((B+p*(N//4))&(N-1))
        for g in range(G):
            rows=slice(p*H,(p+1)*H); src=slice(g*H,(g+1)*H)
            ca[g,rows,:]=cA[src]; sa[g,rows,:]=sA[src]
            cb[g,rows,:]=cB[src]; sb[g,rows,:]=sB[src]

def gen(dst, ca, sa, a0, cb, sb, cref, c0):
    for i in range(AC):
        for r in range(0,R,32):
            A=ca[r:r+32,a0+i:a0+i+1]; S=sa[r:r+32,a0+i:a0+i+1]
            base=A*cb[r:r+32,:]-S*sb[r:r+32,:]
            for t in range(TAPS):
                co=cref[t:t+1,c0+i*128:c0+(i+1)*128]
                dst[t*R+r:t*R+r+32,i*128:(i+1)*128]=(base*co).astype(bf16)

def dots(T, vs, c0, acc):
    if MODE=='stack':
        for f in range(4):
            d=lax.dot_general(T[...],vs[f][:,c0:c0+KC],(((1,),(1,)),((),())),preferred_element_type=f32)
            for t in range(4):
                acc[f+3-t]+=d[t*R:(t+1)*R]
    else:
        for q in range(7):
            s=None
            for f in range(4):
                t=f+3-q
                if 0<=t<4:
                    d=lax.dot_general(T[t*R:(t+1)*R],vs[f][:,c0:c0+KC],(((1,),(1,)),((),())),preferred_element_type=f32)
                    s=d if s is None else s+d
            acc[q]+=s

def front_kernel(v0,v1,v2,v3,kept,co,scale,own,halo,T0,T1,acc,ca,sa,cb,sb,ra,rs):
    g=pl.program_id(0); s=pl.program_id(1)
    vs=(v0,v1,v2,v3)
    @pl.when((g==0)&(s==0))
    def _():
        init_tables(kept,ca,sa,cb,sb)
        gen(T0,ca[0],sa[0],0,cb[0],sb[0],co.at[:,N-KC:],0)
    @pl.when(s==0)
    def _(): acc[...]=jnp.zeros_like(acc)
    nxt=lax.rem(g+(s+1)//STEPS,G)
    shift=lax.rem(128-(2*AC*s+AC),128)
    ra[...]=pltpu.roll(ca[g],shift,1)
    rs[...]=pltpu.roll(sa[g],shift,1)
    c1=co.at[:,pl.ds(pl.multiple_of(s*2*KC,2*KC),2*KC)]
    gen(T1,ra,rs,0,cb[g],sb[g],c1,0)
    dots(T0,vs,0,acc)
    if G>1:
        ra[...]=pltpu.roll(ca[nxt],shift,1)
        rs[...]=pltpu.roll(sa[nxt],shift,1)
    gen(T0,ra,rs,AC,cb[nxt],sb[nxt],c1,KC)
    dots(T1,vs,KC,acc)
    @pl.when(s==STEPS-1)
    def _():
        sc=scale[...].astype(f32)*np.float32(1/16/np.sqrt(N))
        for q in range(1,5): own[0,q-1]=acc[q]*sc
        for i,q in enumerate((5,6,0)): halo[0,i]=(acc[q]*sc).astype(bf16)

def raw(volt, scale_codes, kept):
    c=prototype()
    cs=jnp.asarray(np.roll(c,-KC,axis=1))
    kept=kept.reshape(32,G,4//G).transpose(1,0,2).reshape(1,128)
    vspec=[pl.BlockSpec((256,2*KC),functools.partial(lambda f,g,s:(0,f*STEPS+s),f)) for f in range(4)]
    full=lambda s: pl.BlockSpec(s,lambda g,i:(0,)*len(s))
    return pl.pallas_call(front_kernel,
        grid=(G,STEPS),
        in_specs=vspec+[full((1,128)),full((4,N)),full((1,256))],
        out_specs=[pl.BlockSpec((1,4,R,256),lambda g,s:(g,0,0,0)),pl.BlockSpec((1,3,R,256),lambda g,s:(g,0,0,0))],
        out_shape=[jax.ShapeDtypeStruct((G,4,R,256),f32),jax.ShapeDtypeStruct((G,3,R,256),bf16)],
        scratch_shapes=[pltpu.VMEM((4*R,KC),bf16),pltpu.VMEM((4*R,KC),bf16),pltpu.VMEM((7,R,256),f32)]
            +[pltpu.VMEM((G,R,128),f32)]*4+[pltpu.VMEM((R,128),f32)]*2,
        compiler_params=pltpu.CompilerParams(vmem_limit_bytes=60000*1024),
        name="front",
    )(volt,volt,volt,volt,kept,cs,scale_codes[None,:])


MESH=pl.DeviceIdType.MESH
NC=32

def comm_kernel(variant, own, halo, every, W, S, rh, hs, hr, ss, rs, fs, fr):
    me_i=lax.axis_index("inp"); me=lax.axis_index("chan")
    core=lax.rem(me_i,2); zlo=me_i//2
    nxt=lax.rem(me+1,NC); prv=lax.rem(me+NC-1,NC)
    bar=pltpu.get_barrier_semaphore()
    def peers(fn):
        def body(k,carry):
            c2=lax.rem(me+k,NC)
            fn(k,me_i,c2)
            return carry
        lax.fori_loop(1,NC,body,0)
    def sig(i2,c2): pl.semaphore_signal(bar,inc=1,device_id=(i2,c2),device_id_type=MESH)
    other=(1-zlo)*2+core
    partner=zlo*2+1-core
    def b1(k,carry):
        c2=lax.rem(me+k,NC)
        sig(me_i,c2)
        return carry
    lax.fori_loop(1,NC,b1,0)
    n=NC-1
    if variant=='D':
        def b2(k,carry):
            c2=lax.rem(me+k,NC)
            sig(other,c2)
            return carry
        lax.fori_loop(0,NC,b2,0)
        n+=NC
    else:
        sig(other,me); n+=1
    sig(partner,me); n+=1
    pl.semaphore_wait(bar,n)
    cf=pltpu.make_async_remote_copy(halo.at[pl.ds(0,2)],rh.at[pl.ds(0,2)],hs.at[0],hr.at[0],device_id=(me_i,nxt),device_id_type=MESH)
    cb=pltpu.make_async_remote_copy(halo.at[2],rh.at[2],hs.at[1],hr.at[1],device_id=(me_i,prv),device_id_type=MESH)
    cf.start(); cb.start()
    cf.wait(); cb.wait()
    first=(me>0).astype(f32); last=(me<NC-1).astype(f32)
    parts=(own[0]+rh[0].astype(f32)*first,own[1]+rh[1].astype(f32)*first,own[2],own[3]*last+rh[2].astype(f32))
    for s in range(4):
        for h in range(2):
            for p in range(2):
                W[h,pl.ds(p*4+s,128,stride=8),:]=parts[s][p*128:(p+1)*128,h*128:(h+1)*128]
    for h in range(2):
        S[:,:,h*128:(h+1)*128]=W[h].astype(bf16).reshape(32,32,128)
    lc=pltpu.make_async_copy(S.at[me],every.at[me_i,me],fs.at[2,0])
    lc.start()
    def send(z,k,i2,c2):
        return pltpu.make_async_remote_copy(S.at[c2],every.at[me_i,me],ss.at[z,k],rs.at[z,k],device_id=(i2,c2),device_id_type=MESH)
    def s1(k,carry):
        c2=lax.rem(me+k,NC)
        if variant=='D': send(1,k,other,c2).start()
        send(0,k,me_i,c2).start()
        return carry
    if variant=='D': send(1,0,other,me).start()
    lax.fori_loop(1,NC,s1,0)
    lc.wait()
    def fwd(z,i_src,k,target,sem):
        c1=lax.rem(me+NC-k,NC)
        return pltpu.make_async_remote_copy(every.at[i_src,c1],every.at[i_src,c1],fs.at[sem,k],fr.at[sem,k],device_id=(target,me),device_id_type=MESH)
    def recv_wait(z,k,i_src):
        c1=lax.rem(me+NC-k,NC)
        pltpu.make_async_remote_copy(S.at[0],every.at[i_src,c1],ss.at[z,k],rs.at[z,k],device_id=(me_i,me),device_id_type=MESH).wait_recv()
    if variant=='D':
        fwd(0,me_i,0,partner,0).start()
        recv_wait(1,0,other); fwd(1,other,0,partner,1).start()
        def a1(k,carry):
            recv_wait(0,k,me_i); fwd(0,me_i,k,partner,0).start()
            recv_wait(1,k,other); fwd(1,other,k,partner,1).start()
            return carry
        lax.fori_loop(1,NC,a1,0)
        po=(1-zlo)*2+1-core
        def e1(k,carry):
            f0=fwd(0,me_i,k,partner,0); f1=fwd(1,other,k,partner,1)
            f0.wait_send(); f1.wait_send()
            fwd(0,partner,k,partner,0).wait_recv(); fwd(1,po,k,partner,1).wait_recv()
            return carry
        lax.fori_loop(0,NC,e1,0)
    else:
        def a0(k):
            fwd(0,me_i,k,other,1).start(); fwd(0,me_i,k,partner,0).start()
        a0(0)
        def a1(k,carry):
            recv_wait(0,k,me_i); a0(k)
            return carry
        lax.fori_loop(1,NC,a1,0)
        def a2(k,carry):
            fwd(0,other,k,other,1).wait_recv(); fwd(0,other,k,partner,2).start()
            return carry
        lax.fori_loop(0,NC,a2,0)
        po=(1-zlo)*2+1-core
        def e1(k,carry):
            fwd(0,me_i,k,other,1).wait_send(); fwd(0,me_i,k,partner,0).wait_send(); fwd(0,other,k,partner,2).wait_send()
            fwd(0,partner,k,partner,0).wait_recv(); fwd(0,po,k,partner,2).wait_recv()
            return carry
        lax.fori_loop(0,NC,e1,0)
    def e2(k,carry):
        send(0,k,me_i,me).wait_send()
        if variant=='D': send(1,k,me_i,me).wait_send()
        return carry
    lax.fori_loop(1,NC,e2,0)
    if variant=='D': send(1,0,other,me).wait_send()

def comm(own,halo,variant='D',cid=0):
    vm=pl.BlockSpec(memory_space=pltpu.VMEM)
    DMA=pltpu.SemaphoreType.DMA
    return pl.pallas_call(functools.partial(comm_kernel,variant),
        in_specs=[vm,vm],out_specs=vm,
        out_shape=jax.ShapeDtypeStruct((4,32,32,256),bf16),
        scratch_shapes=[pltpu.VMEM((2,1024,128),f32),pltpu.VMEM((32,32,256),bf16),pltpu.VMEM((3,256,256),bf16),
            DMA((2,)),DMA((2,)),DMA((2,NC)),DMA((2,NC)),DMA((3,NC)),DMA((3,NC))],
        compiler_params=pltpu.CompilerParams(collective_id=cid,has_side_effects=True,vmem_limit_bytes=40*1024*1024),
        name="comm"+variant)(own,halo)

def correlate_kernel(every,out):
    a=every[lax.axis_index('inp')].astype(f32)
    turned=jnp.concatenate([a[:,4:],-a[:,:4]],axis=1)
    both=jnp.concatenate([a.reshape(256,256),turned.reshape(256,256)],axis=1).astype(bf16)
    for i in range(4):
        b=every[i].astype(f32).reshape(256,256).astype(bf16)
        d=lax.dot_general(both,b,(((0,),(0,)),((),())),preferred_element_type=f32)*np.float32(1/128)
        out[0,0,:,i*256:(i+1)*256]=d[:256]
        out[1,0,:,i*256:(i+1)*256]=d[256:]

def correlate(every):
    return pl.pallas_call(correlate_kernel,
        grid=(4,),
        in_specs=[pl.BlockSpec((4,32,8,256),lambda j:(0,0,j,0))],
        out_specs=pl.BlockSpec((2,1,256,1024),lambda j:(0,j,0,0)),
        out_shape=jax.ShapeDtypeStruct((2,4,256,1024),f32),
        compiler_params=pltpu.CompilerParams(vmem_limit_bytes=40*1024*1024),
        name="correlate")(every)


def local(voltages,scale_codes,kept_channels):
    own,halo=raw(voltages,scale_codes,kept_channels)
    return correlate(comm(own[0],halo[0],'P'))

def solution(mesh):
    placed=(P("inp","chan"),P("inp"),P())
    return jax.shard_map(local,mesh=mesh,in_specs=placed,out_specs=P(None,"chan","inp",None),check_vma=False)
```

```python
import functools
import numpy as np
import jax
import jax.numpy as jnp
from jax import lax
from jax.experimental import pallas as pl
from jax.experimental.pallas import tpu as pltpu
from jax.sharding import PartitionSpec as P

N = 8192
TAPS = 4
KC = 512
CHUNKS = N // KC
PAIRS = CHUNKS // 2
AC = KC // 128
NC = 32
ROWS = 256
LOAD = 1024
f32 = jnp.float32
bf16 = jnp.bfloat16
MESH = pl.DeviceIdType.MESH
ORDER = (3, 2, 4, 1)
UNROLL = 4
RUNS = CHUNKS // UNROLL
DIRECT = (2, 3)


def prototype():
    m = np.arange(TAPS * N, dtype=np.float64)
    u = (m + 0.5) / N - TAPS / 2
    w = 0.5 - 0.5 * np.cos(2 * np.pi * (m + 0.5) / (TAPS * N))
    return (np.sinc(u) * w).reshape(TAPS, N).astype(np.float32)


def cos_sin(m):
    quad = (m + N // 8) // (N // 4)
    x = (m - quad * (N // 4)).astype(f32) * np.float32(2 * np.pi / N)
    y = x * x
    c = 1.0 + y * (-0.5 + y * (1 / 24 + y * (-1 / 720 + y * (1 / 40320))))
    s = x * (1.0 + y * (-1 / 6 + y * (1 / 120 + y * (-1 / 5040 + y * (1 / 362880)))))
    quad = quad & 3
    odd = (quad & 1) == 1
    cc = jnp.where(odd, s, c)
    ss = jnp.where(odd, c, s)
    cc = jnp.where((quad == 1) | (quad == 2), -cc, cc)
    ss = jnp.where(quad >= 2, -ss, ss)
    return cc, ss


def init_tables(kept, ca, sa, cb, sb):
    kt = jnp.transpose(jnp.broadcast_to(kept[...].astype(f32), (128, 128)))
    kt = kt.reshape(32, 4, 128)
    kt = jnp.concatenate([kt, kt], axis=1).reshape(ROWS, 128).astype(jnp.int32)
    lane = lax.broadcasted_iota(jnp.int32, (ROWS, 128), 1)
    row = lax.broadcasted_iota(jnp.int32, (ROWS, 128), 0)
    ca[...], sa[...] = cos_sin((kt * ((lane & 63) * 128)) & (N - 1))
    cb[...], sb[...] = cos_sin((kt * lane + ((row >> 2) & 1) * (N // 4)) & (N - 1))


def gen(stage, full, chunk, ca, sa, a0, cb, sb, co):
    for i in range(AC):
        off = pl.multiple_of(chunk * KC + i * 128, 128)
        for r in range(0, ROWS, 32):
            base = ca[r : r + 32, a0 + i : a0 + i + 1] * cb[r : r + 32, :]
            base = base - sa[r : r + 32, a0 + i : a0 + i + 1] * sb[r : r + 32, :]
            for t in range(TAPS):
                val = (base * co[t : t + 1, pl.ds(off, 128)]).astype(bf16)
                stage[t, r : r + 32, i * 128 : (i + 1) * 128] = val
                full[chunk, t, r : r + 32, i * 128 : (i + 1) * 128] = val


def product(table, V, f, chunk):
    v = V[f, :, pl.ds(pl.multiple_of(chunk * KC, KC), KC)]
    return lax.dot_general(table, v, (((1,), (1,)), ((), ())), preferred_element_type=f32)


def terms(q):
    return [(f, f + 3 - q) for f in range(4) if 0 <= f + 3 - q < 4]


def mega_kernel(volt, kept, co, codes, out, every, V, T, T0, T1, acc, ca, sa, cb, sb, ra, rs,
                HS, HR, S, vsem, hs, hr, ss, rcv, ds, dr, fs, fr, own, done):
    me_i = lax.axis_index("inp")
    me = lax.axis_index("chan")
    core = lax.rem(me_i, 2)
    zlo = me_i // 2
    other = (1 - zlo) * 2 + core
    partner = zlo * 2 + 1 - core
    across = (1 - zlo) * 2 + 1 - core
    nxt = lax.rem(me + 1, NC)
    prv = lax.rem(me + NC - 1, NC)
    loads = N // LOAD

    def load(f, k):
        off = pl.multiple_of(k * LOAD, LOAD)
        return pltpu.make_async_copy(
            volt.at[:, pl.ds(pl.multiple_of(f * N + off, LOAD), LOAD)],
            V.at[f, :, pl.ds(off, LOAD)], vsem.at[f, k])

    def start_loads(k, carry):
        for f in (2, 3):
            load(f, k).start()
        return carry

    lax.fori_loop(0, loads, start_loads, 0)
    for f in (0, 1):
        lax.fori_loop(0, loads, lambda k, c: (load(f, k).start(), c)[1], 0)

    bar = pltpu.get_barrier_semaphore()

    def greet(k, carry):
        pl.semaphore_signal(bar, inc=1, device_id=(me_i, lax.rem(me + k, NC)), device_id_type=MESH)
        return carry

    lax.fori_loop(1, NC, greet, 0)

    def greet_other(k, carry):
        pl.semaphore_signal(bar, inc=1, device_id=(other, lax.rem(me + k, NC)), device_id_type=MESH)
        return carry

    lax.fori_loop(1, NC, greet_other, 0)
    pl.semaphore_signal(bar, inc=1, device_id=(other, me), device_id_type=MESH)
    pl.semaphore_signal(bar, inc=1, device_id=(partner, me), device_id_type=MESH)

    init_tables(kept, ca, sa, cb, sb)
    gen(T0, T, 0, ca, sa, 0, cb, sb, co)
    acc[...] = jnp.zeros_like(acc)

    def edge_dots(stage, chunk):
        for q in (5, 6):
            acc[q] += sum(product(stage[t], V, f, chunk) for f, t in terms(q))

    def edge_step(s, carry):
        for f in (2, 3):
            load(f, s).wait()
        shift = lax.rem(128 - (2 * AC * s + AC), 128)
        ra[...] = pltpu.roll(ca[...], shift, 1)
        rs[...] = pltpu.roll(sa[...], shift, 1)
        gen(T1, T, 2 * s + 1, ra, rs, 0, cb, sb, co)
        edge_dots(T0, 2 * s)
        gen(T0, T, lax.rem(2 * s + 2, CHUNKS), ra, rs, AC, cb, sb, co)
        edge_dots(T1, 2 * s + 1)
        return carry

    lax.fori_loop(0, PAIRS, edge_step, 0)
    sc = codes[...].astype(f32) * np.float32(1 / 16 / np.sqrt(N))
    for i, q in enumerate((5, 6)):
        HS[i] = (acc[q] * sc).astype(bf16)
    pl.semaphore_wait(bar, 2 * NC)
    fwd = pltpu.make_async_remote_copy(
        HS.at[pl.ds(0, 2)], HR.at[pl.ds(0, 2)], hs.at[0], hr.at[0],
        device_id=(me_i, nxt), device_id_type=MESH)
    fwd.start()

    def run(q, lo, hi):
        def step(s, carry):
            acc[q] += sum(
                product(T[UNROLL * s + h, t], V, f, UNROLL * s + h) for h in range(UNROLL) for f, t in terms(q))
            return carry
        lax.fori_loop(lo, hi, step, 0)

    lax.fori_loop(0, loads, lambda k, c: (load(0, k).wait(), c)[1], 0)
    run(0, 0, RUNS)
    HS[2] = (acc[0] * sc).astype(bf16)
    bwd = pltpu.make_async_remote_copy(
        HS.at[2], HR.at[2], hs.at[1], hr.at[1], device_id=(me_i, prv), device_id_type=MESH)
    bwd.start()
    lax.fori_loop(0, loads, lambda k, c: (load(1, k).wait(), c)[1], 0)

    def keep_own(slot):
        return pltpu.make_async_copy(S.at[slot, me], every.at[slot, me_i, me], own.at[slot])

    def publish(slot):
        q = ORDER[slot]
        part = acc[q] * sc
        if q == 1:
            part += HR[0].astype(f32) * (me > 0).astype(f32)
        elif q == 2:
            part += HR[1].astype(f32) * (me > 0).astype(f32)
        elif q == 4:
            part = part * (me < NC - 1).astype(f32) + HR[2].astype(f32)
        S[slot] = part.astype(bf16).reshape(NC, 8, 256)
        keep_own(slot).start()

        if slot in DIRECT:
            direct(slot, me).start()

        def send(k, carry):
            to = lax.rem(me + k, NC)
            if slot in DIRECT:
                direct(slot, to).start()
            pltpu.make_async_remote_copy(
                S.at[slot, to], every.at[slot, me_i, me], ss.at[slot], rcv.at[slot],
                device_id=(me_i, to), device_id_type=MESH).start()
            return carry

        lax.fori_loop(1, NC, send, 0)

    def direct(slot, to):
        return pltpu.make_async_remote_copy(
            S.at[slot, to], every.at[slot, me_i, me], ds.at[slot], dr.at[slot],
            device_id=(other, to), device_id_type=MESH)

    def arrivals(slot):
        rest = pl.ds(0, NC - 1)
        return pltpu.make_async_remote_copy(
            S.at[slot, rest], every.at[slot, me_i, rest], ss.at[slot], rcv.at[slot],
            device_id=(other, me), device_id_type=MESH)

    def arrivals_other(slot):
        return pltpu.make_async_remote_copy(
            S.at[slot], every.at[slot, other], ds.at[slot], dr.at[slot],
            device_id=(other, me), device_id_type=MESH)

    def pass_on(slot, kind, who, to):
        block = every.at[slot, who]
        return pltpu.make_async_remote_copy(
            block, block, fs.at[slot, kind], fr.at[slot, kind],
            device_id=(to, me), device_id_type=MESH)

    def forward(slot):
        keep_own(slot).wait()
        arrivals(slot).wait_recv()
        if slot not in DIRECT:
            pass_on(slot, 0, me_i, other).start()
        pass_on(slot, 1, me_i, partner).start()

    def relay(slot):
        if slot in DIRECT:
            arrivals_other(slot).wait_recv()
        else:
            pass_on(slot, 0, other, other).wait_recv()
        pass_on(slot, 2, other, partner).start()

    def store(slot):
        return pltpu.make_async_copy(every.at[slot], out.at[slot], done.at[slot])

    def finish(slot):
        pass_on(slot, 1, partner, partner).wait_recv()
        pass_on(slot, 2, across, partner).wait_recv()
        store(slot).start()

    run(3, 0, RUNS)
    publish(0)
    run(2, 0, RUNS)
    fwd.wait()
    bwd.wait()
    publish(1)
    run(4, 0, 1)
    forward(0)
    run(4, 1, RUNS)
    publish(2)
    run(1, 0, RUNS // 2)
    forward(1)
    relay(0)
    run(1, RUNS // 2, RUNS)
    publish(3)
    relay(1)
    finish(0)
    forward(2)
    relay(2)
    finish(1)
    forward(3)
    relay(3)
    finish(2)
    finish(3)
    for slot in range(4):
        arrivals(slot).wait_send()
        if slot in DIRECT:
            arrivals_other(slot).wait_send()
        else:
            pass_on(slot, 0, me_i, other).wait_send()
        pass_on(slot, 1, me_i, partner).wait_send()
        pass_on(slot, 2, other, partner).wait_send()
        store(slot).wait()


def mega(volt, scale_codes, kept):
    vm = pl.BlockSpec(memory_space=pltpu.VMEM)
    DMA = pltpu.SemaphoreType.DMA
    VM = pltpu.VMEM
    return pl.pallas_call(
        mega_kernel,
        in_specs=[pl.BlockSpec(memory_space=pl.ANY), vm, vm, vm],
        out_specs=pl.BlockSpec(memory_space=pl.ANY),
        out_shape=jax.ShapeDtypeStruct((4, 4, NC, 8, 256), bf16),
        scratch_shapes=[
            VM((4, 4, NC, 8, 256), bf16),
            VM((4, 256, N), bf16), VM((CHUNKS, TAPS, ROWS, KC), bf16),
            VM((TAPS, ROWS, KC), bf16), VM((TAPS, ROWS, KC), bf16), VM((7, ROWS, 256), f32),
            VM((ROWS, 128), f32), VM((ROWS, 128), f32), VM((ROWS, 128), f32), VM((ROWS, 128), f32),
            VM((ROWS, 128), f32), VM((ROWS, 128), f32),
            VM((3, ROWS, 256), bf16), VM((3, ROWS, 256), bf16), VM((4, NC, 8, 256), bf16),
            DMA((4, N // LOAD)), DMA((2,)), DMA((2,)), DMA((4,)), DMA((4,)), DMA((4,)), DMA((4,)), DMA((4, 3)), DMA((4, 3)), DMA((4,)), DMA((4,)),
        ],
        compiler_params=pltpu.CompilerParams(
            collective_id=0, has_side_effects=True, vmem_limit_bytes=60000 * 1024),
        name="mega",
    )(volt, kept[None, :], jnp.asarray(prototype()), scale_codes[None, :])


def correlate_kernel(where, every, out, F, A):
    step = pl.program_id(0)
    for h in range(2):
        F[h] = every[:, 0, :, :, h * 128 : (h + 1) * 128].astype(f32).reshape(1024, 128)

    def rows(j, p):
        return jnp.concatenate(
            [F[h, pl.ds(p * 4 + j, 128, stride=8), :] for h in range(2)], axis=1)

    @pl.when(step == 0)
    def _():
        for j in range(4):
            re = jnp.transpose(rows(j, 0))
            im = jnp.transpose(rows(j, 1))
            A[j, :256, :128] = re.astype(bf16)
            A[j, :256, 128:] = im.astype(bf16)
            A[j, 256:, :128] = im.astype(bf16)
            A[j, 256:, 128:] = (-re).astype(bf16)

    for j in range(4):
        b = jnp.concatenate([rows(j, 0), rows(j, 1)], axis=0).astype(bf16)
        d = jnp.dot(A[j], b, preferred_element_type=f32) * np.float32(1 / 128)
        out[0, j] = d[:256]
        out[1, j] = d[256:]


def correlate(every):
    where = lax.axis_index("inp").astype(jnp.int32)[None]
    return pl.pallas_call(
        correlate_kernel,
        grid_spec=pltpu.PrefetchScalarGridSpec(
            num_scalar_prefetch=1,
            grid=(4,),
            in_specs=[pl.BlockSpec((4, 1, NC, 8, 256), lambda i, w: (0, lax.rem(w[0] + i, 4), 0, 0, 0))],
            out_specs=pl.BlockSpec((2, 4, 256, 256), lambda i, w: (0, 0, 0, lax.rem(w[0] + i, 4))),
            scratch_shapes=[pltpu.VMEM((2, 1024, 128), f32), pltpu.VMEM((4, 512, 256), bf16)],
        ),
        out_shape=jax.ShapeDtypeStruct((2, 4, 256, 1024), f32),
        compiler_params=pltpu.CompilerParams(vmem_limit_bytes=60000 * 1024),
        name="correlate",
    )(where, every)


def local(voltages, scale_codes, kept_channels):
    return correlate(mega(voltages, scale_codes, kept_channels))


def solution(mesh):
    placed = (P("inp", "chan"), P("inp"), P())
    return jax.shard_map(
        local, mesh=mesh, in_specs=placed, out_specs=P(None, "chan", "inp", None), check_vma=False)
```

```python
import functools
import numpy as np
import jax
import jax.numpy as jnp
from jax import lax
from jax.experimental import pallas as pl
from jax.experimental.pallas import tpu as pltpu
from jax.sharding import PartitionSpec as P

N = 8192
TAPS = 4
KC = 512
CHUNKS = N // KC
PAIRS = CHUNKS // 2
AC = KC // 128
NC = 32
ROWS = 256
LOAD = 1024
f32 = jnp.float32
bf16 = jnp.bfloat16
MESH = pl.DeviceIdType.MESH
ORDER = (3, 2, 4, 1)
UNROLL = 4
RUNS = CHUNKS // UNROLL
DIRECT = (2, 3)


def prototype():
    m = np.arange(TAPS * N, dtype=np.float64)
    u = (m + 0.5) / N - TAPS / 2
    w = 0.5 - 0.5 * np.cos(2 * np.pi * (m + 0.5) / (TAPS * N))
    return (np.sinc(u) * w).reshape(TAPS, N).astype(np.float32)


def cos_sin(m):
    quad = (m + N // 8) // (N // 4)
    x = (m - quad * (N // 4)).astype(f32) * np.float32(2 * np.pi / N)
    y = x * x
    c = 1.0 + y * (-0.5 + y * (1 / 24 + y * (-1 / 720 + y * (1 / 40320))))
    s = x * (1.0 + y * (-1 / 6 + y * (1 / 120 + y * (-1 / 5040 + y * (1 / 362880)))))
    quad = quad & 3
    odd = (quad & 1) == 1
    cc = jnp.where(odd, s, c)
    ss = jnp.where(odd, c, s)
    cc = jnp.where((quad == 1) | (quad == 2), -cc, cc)
    ss = jnp.where(quad >= 2, -ss, ss)
    return cc, ss


def init_tables(kept, ca, sa, cb, sb):
    kt = jnp.transpose(jnp.broadcast_to(kept[...].astype(f32), (128, 128)))
    kt = kt.reshape(32, 4, 128)
    kt = jnp.concatenate([kt, kt], axis=1).reshape(ROWS, 128).astype(jnp.int32)
    lane = lax.broadcasted_iota(jnp.int32, (ROWS, 128), 1)
    row = lax.broadcasted_iota(jnp.int32, (ROWS, 128), 0)
    ca[...], sa[...] = cos_sin((kt * ((lane & 63) * 128)) & (N - 1))
    cb[...], sb[...] = cos_sin((kt * lane + ((row >> 2) & 1) * (N // 4)) & (N - 1))


def gen(stage, full, chunk, ca, sa, a0, cb, sb, co):
    for i in range(AC):
        off = pl.multiple_of(chunk * KC + i * 128, 128)
        for r in range(0, ROWS, 32):
            base = ca[r : r + 32, a0 + i : a0 + i + 1] * cb[r : r + 32, :]
            base = base - sa[r : r + 32, a0 + i : a0 + i + 1] * sb[r : r + 32, :]
            for t in range(TAPS):
                val = (base * co[t : t + 1, pl.ds(off, 128)]).astype(bf16)
                stage[t, r : r + 32, i * 128 : (i + 1) * 128] = val
                full[chunk, t, r : r + 32, i * 128 : (i + 1) * 128] = val


def product(table, V, f, chunk):
    v = V[f, :, pl.ds(pl.multiple_of(chunk * KC, KC), KC)]
    return lax.dot_general(table, v, (((1,), (1,)), ((), ())), preferred_element_type=f32)


def terms(q):
    return [(f, f + 3 - q) for f in range(4) if 0 <= f + 3 - q < 4]


def mega_kernel(volt, kept, co, codes, out, every, V, T, T0, T1, acc, ca, sa, cb, sb, ra, rs,
                HS, HR, S, vsem, hs, hr, ss, rcv, ds, dr, fs, fr, own, done):
    me_i = lax.axis_index("inp")
    me = lax.axis_index("chan")
    core = lax.rem(me_i, 2)
    zlo = me_i // 2
    other = (1 - zlo) * 2 + core
    partner = zlo * 2 + 1 - core
    across = (1 - zlo) * 2 + 1 - core
    nxt = lax.rem(me + 1, NC)
    prv = lax.rem(me + NC - 1, NC)
    loads = N // LOAD

    def load(f, k):
        off = pl.multiple_of(k * LOAD, LOAD)
        return pltpu.make_async_copy(
            volt.at[:, pl.ds(pl.multiple_of(f * N + off, LOAD), LOAD)],
            V.at[f, :, pl.ds(off, LOAD)], vsem.at[f, k])

    def start_loads(k, carry):
        for f in (2, 3):
            load(f, k).start()
        return carry

    lax.fori_loop(0, loads, start_loads, 0)
    for f in (0, 1):
        lax.fori_loop(0, loads, lambda k, c: (load(f, k).start(), c)[1], 0)

    bar = pltpu.get_barrier_semaphore()

    def greet(k, carry):
        pl.semaphore_signal(bar, inc=1, device_id=(me_i, lax.rem(me + k, NC)), device_id_type=MESH)
        return carry

    lax.fori_loop(1, NC, greet, 0)

    def greet_other(k, carry):
        pl.semaphore_signal(bar, inc=1, device_id=(other, lax.rem(me + k, NC)), device_id_type=MESH)
        return carry

    lax.fori_loop(1, NC, greet_other, 0)
    pl.semaphore_signal(bar, inc=1, device_id=(other, me), device_id_type=MESH)
    pl.semaphore_signal(bar, inc=1, device_id=(partner, me), device_id_type=MESH)

    init_tables(kept, ca, sa, cb, sb)
    gen(T0, T, 0, ca, sa, 0, cb, sb, co)
    acc[...] = jnp.zeros_like(acc)

    def edge_dots(stage, chunk):
        for q in (5, 6):
            acc[q] += sum(product(stage[t], V, f, chunk) for f, t in terms(q))

    def edge_step(s, carry):
        for f in (2, 3):
            load(f, s).wait()
        shift = lax.rem(128 - (2 * AC * s + AC), 128)
        ra[...] = pltpu.roll(ca[...], shift, 1)
        rs[...] = pltpu.roll(sa[...], shift, 1)
        gen(T1, T, 2 * s + 1, ra, rs, 0, cb, sb, co)
        edge_dots(T0, 2 * s)
        gen(T0, T, lax.rem(2 * s + 2, CHUNKS), ra, rs, AC, cb, sb, co)
        edge_dots(T1, 2 * s + 1)
        return carry

    lax.fori_loop(0, PAIRS, edge_step, 0)
    sc = codes[...].astype(f32) * np.float32(1 / 16 / np.sqrt(N))
    for i, q in enumerate((5, 6)):
        HS[i] = (acc[q] * sc).astype(bf16)
    pl.semaphore_wait(bar, 2 * NC)
    fwd = pltpu.make_async_remote_copy(
        HS.at[pl.ds(0, 2)], HR.at[pl.ds(0, 2)], hs.at[0], hr.at[0],
        device_id=(me_i, nxt), device_id_type=MESH)
    fwd.start()

    def run(q, lo, hi):
        def step(s, carry):
            acc[q] += sum(
                product(T[UNROLL * s + h, t], V, f, UNROLL * s + h) for h in range(UNROLL) for f, t in terms(q))
            return carry
        lax.fori_loop(lo, hi, step, 0)

    lax.fori_loop(0, loads, lambda k, c: (load(0, k).wait(), c)[1], 0)
    run(0, 0, RUNS)
    HS[2] = (acc[0] * sc).astype(bf16)
    bwd = pltpu.make_async_remote_copy(
        HS.at[2], HR.at[2], hs.at[1], hr.at[1], device_id=(me_i, prv), device_id_type=MESH)
    bwd.start()
    lax.fori_loop(0, loads, lambda k, c: (load(1, k).wait(), c)[1], 0)

    def keep_own(slot):
        return pltpu.make_async_copy(S.at[slot, me], every.at[slot, me_i, me], own.at[slot])

    def publish(slot):
        q = ORDER[slot]
        part = acc[q] * sc
        if q == 1:
            part += HR[0].astype(f32) * (me > 0).astype(f32)
        elif q == 2:
            part += HR[1].astype(f32) * (me > 0).astype(f32)
        elif q == 4:
            part = part * (me < NC - 1).astype(f32) + HR[2].astype(f32)
        S[slot] = part.astype(bf16).reshape(NC, 8, 256)
        keep_own(slot).start()

        if slot in DIRECT:
            direct(slot, me).start()

        def send(k, carry):
            to = lax.rem(me + k, NC)
            if slot in DIRECT:
                direct(slot, to).start()
            pltpu.make_async_remote_copy(
                S.at[slot, to], every.at[slot, me_i, me], ss.at[slot], rcv.at[slot],
                device_id=(me_i, to), device_id_type=MESH).start()
            return carry

        lax.fori_loop(1, NC, send, 0)

    def direct(slot, to):
        return pltpu.make_async_remote_copy(
            S.at[slot, to], every.at[slot, me_i, me], ds.at[slot], dr.at[slot],
            device_id=(other, to), device_id_type=MESH)

    def arrivals(slot):
        rest = pl.ds(0, NC - 1)
        return pltpu.make_async_remote_copy(
            S.at[slot, rest], every.at[slot, me_i, rest], ss.at[slot], rcv.at[slot],
            device_id=(other, me), device_id_type=MESH)

    def arrivals_other(slot):
        return pltpu.make_async_remote_copy(
            S.at[slot], every.at[slot, other], ds.at[slot], dr.at[slot],
            device_id=(other, me), device_id_type=MESH)

    def pass_on(slot, kind, who, to):
        block = every.at[slot, who]
        return pltpu.make_async_remote_copy(
            block, block, fs.at[slot, kind], fr.at[slot, kind],
            device_id=(to, me), device_id_type=MESH)

    def forward(slot):
        keep_own(slot).wait()
        arrivals(slot).wait_recv()
        if slot not in DIRECT:
            pass_on(slot, 0, me_i, other).start()
        pass_on(slot, 1, me_i, partner).start()

    def relay(slot):
        if slot in DIRECT:
            arrivals_other(slot).wait_recv()
        else:
            pass_on(slot, 0, other, other).wait_recv()
        pass_on(slot, 2, other, partner).start()

    def store(slot):
        return pltpu.make_async_copy(every.at[slot], out.at[slot], done.at[slot])

    def finish(slot):
        pass_on(slot, 1, partner, partner).wait_recv()
        pass_on(slot, 2, across, partner).wait_recv()
        store(slot).start()

    run(3, 0, RUNS)
    publish(0)
    run(2, 0, RUNS)
    fwd.wait()
    bwd.wait()
    publish(1)
    run(4, 0, 1)
    forward(0)
    run(4, 1, RUNS)
    publish(2)
    run(1, 0, RUNS // 2)
    forward(1)
    relay(0)
    run(1, RUNS // 2, RUNS)
    publish(3)
    relay(1)
    finish(0)
    forward(2)
    relay(2)
    finish(1)
    forward(3)
    relay(3)
    finish(2)
    finish(3)
    for slot in range(4):
        arrivals(slot).wait_send()
        if slot in DIRECT:
            arrivals_other(slot).wait_send()
        else:
            pass_on(slot, 0, me_i, other).wait_send()
        pass_on(slot, 1, me_i, partner).wait_send()
        pass_on(slot, 2, other, partner).wait_send()
        store(slot).wait()


def mega(volt, scale_codes, kept):
    vm = pl.BlockSpec(memory_space=pltpu.VMEM)
    DMA = pltpu.SemaphoreType.DMA
    VM = pltpu.VMEM
    return pl.pallas_call(
        mega_kernel,
        in_specs=[pl.BlockSpec(memory_space=pl.ANY), vm, vm, vm],
        out_specs=pl.BlockSpec(memory_space=pl.ANY),
        out_shape=jax.ShapeDtypeStruct((4, 4, NC, 8, 256), bf16),
        scratch_shapes=[
            VM((4, 4, NC, 8, 256), bf16),
            VM((4, 256, N), bf16), VM((CHUNKS, TAPS, ROWS, KC), bf16),
            VM((TAPS, ROWS, KC), bf16), VM((TAPS, ROWS, KC), bf16), VM((7, ROWS, 256), f32),
            VM((ROWS, 128), f32), VM((ROWS, 128), f32), VM((ROWS, 128), f32), VM((ROWS, 128), f32),
            VM((ROWS, 128), f32), VM((ROWS, 128), f32),
            VM((3, ROWS, 256), bf16), VM((3, ROWS, 256), bf16), VM((4, NC, 8, 256), bf16),
            DMA((4, N // LOAD)), DMA((2,)), DMA((2,)), DMA((4,)), DMA((4,)), DMA((4,)), DMA((4,)), DMA((4, 3)), DMA((4, 3)), DMA((4,)), DMA((4,)),
        ],
        compiler_params=pltpu.CompilerParams(
            collective_id=0, has_side_effects=True, vmem_limit_bytes=46 * 1024 * 1024),
        name="mega",
    )(volt, kept[None, :], jnp.asarray(prototype()), scale_codes[None, :])


def correlate_kernel(where, every, out, F, A):
    step = pl.program_id(0)
    for h in range(2):
        F[h] = every[:, 0, :, :, h * 128 : (h + 1) * 128].astype(f32).reshape(1024, 128)

    def rows(j, p):
        return jnp.concatenate(
            [F[h, pl.ds(p * 4 + j, 128, stride=8), :] for h in range(2)], axis=1)

    @pl.when(step == 0)
    def _():
        for j in range(4):
            re = jnp.transpose(rows(j, 0)) * np.float32(1 / 128)
            im = jnp.transpose(rows(j, 1)) * np.float32(1 / 128)
            A[j, :256, :128] = re.astype(bf16)
            A[j, :256, 128:] = im.astype(bf16)
            A[j, 256:, :128] = im.astype(bf16)
            A[j, 256:, 128:] = (-re).astype(bf16)

    for j in range(4):
        b = jnp.concatenate([rows(j, 0), rows(j, 1)], axis=0).astype(bf16)
        d = jnp.dot(A[j], b, preferred_element_type=f32)
        out[0, j] = d[:256]
        out[1, j] = d[256:]


def correlate(every):
    where = lax.axis_index("inp").astype(jnp.int32)[None]
    return pl.pallas_call(
        correlate_kernel,
        grid_spec=pltpu.PrefetchScalarGridSpec(
            num_scalar_prefetch=1,
            grid=(4,),
            in_specs=[pl.BlockSpec((4, 1, NC, 8, 256), lambda i, w: (0, lax.rem(w[0] + i, 4), 0, 0, 0))],
            out_specs=pl.BlockSpec((2, 4, 256, 256), lambda i, w: (0, 0, 0, lax.rem(w[0] + i, 4))),
            scratch_shapes=[pltpu.VMEM((2, 1024, 128), f32), pltpu.VMEM((4, 512, 256), bf16)],
        ),
        out_shape=jax.ShapeDtypeStruct((2, 4, 256, 1024), f32),
        compiler_params=pltpu.CompilerParams(vmem_limit_bytes=30 * 1024 * 1024),
        name="correlate",
    )(where, every)


def local(voltages, scale_codes, kept_channels):
    return correlate(mega(voltages, scale_codes, kept_channels))


def solution(mesh):
    placed = (P("inp", "chan"), P("inp"), P())
    return jax.shard_map(
        local, mesh=mesh, in_specs=placed, out_specs=P(None, "chan", "inp", None), check_vma=False)
```
